32 devices in a mesh: slide: 2 (over x), col: 16 (over z, y, core).
Axes of the slice: x: 2, y: 2, z: 4, core: 2. Of those that a mesh axis runs over, the one named last changes fastest.
Arguments:
- patches: bfloat16 [256, 128, 512], P(('slide', 'col')), parts along dimension 0, may hold values from -6 to 6
- tissue: int32 [256, 128], P(('slide', 'col')), parts along dimension 0, may hold values from 0 to 1, as said below
- w_query: bfloat16 [512, 512], replicated, may hold values from -0.25 to 0.25
- w_key: bfloat16 [512, 512], replicated, may hold values from -0.25 to 0.25
- w_value: bfloat16 [512, 512], replicated, may hold values from -0.25 to 0.25
- w_out: bfloat16 [512, 512], replicated, may hold values from -0.25 to 0.25
- agent_tokens: bfloat16 [256, 512], replicated, may hold values from -100 to 100
- kernel_seven: float32 [7, 7, 512], replicated, may hold values from -0.875 to 0.875
- kernel_five: float32 [5, 5, 512], replicated, may hold values from -1.25 to 1.25
- kernel_three: float32 [3, 3, 512], replicated, may hold values from -2 to 2
Outputs:
- mixed: bfloat16 [256, 128, 512], P(('slide', 'col')), parts along dimension 0
The draws below stay inside these ranges and needn't reach their ends.
There are 2 independent parts, one for each index of `slide`. The reference program is written for one: setup_inputs(seed, part) draws one part's arguments, and reference() takes and returns one part's arrays. A program takes and returns all parts, laid end to end along the dimension named above; an argument that names none is the same for every part. Nothing has to cross between parts.
Inputs may be any that keep to these rules, and one draw needn't show every extreme that they name: tissue holds 0 or 1; each slide has at least one tissue patch.
All inputs are finite; a program needn't handle non-finite values.
Results may differ from the reference program's by a relative error of at most 0.007.
The reference program's roundings to bfloat16 on the way (of `agent_values`, `token_weights` and `blended`) count: a program that leaves them out, or rounds other values in their place, can miss the bound.
Values may be sent and summed in bfloat16 or wider, within the bound.
A program may use at most 128 MiB of HBM per device.

```python
import jax
import jax.numpy as jnp
from jax import lax

D = 512
HEADS = 8
HEAD_DIM = 64
AGENTS = 256
GRID_W = 128
ROWS_DEV = 8
GRID_H = 128
N_COL = 16


def draw_tissue(key, part):
    subkeys = jax.random.split(key, 4)
    side_cells = min(GRID_H, GRID_W)
    center_rows = jax.random.randint(subkeys[0], (8,), 0, GRID_H)
    center_cols = jax.random.randint(subkeys[1], (8,), 0, GRID_W)
    radii = jax.random.randint(subkeys[2], (8,), max(side_cells // 8, 1), side_cells // 4 + 1)
    row_ids = jnp.arange(GRID_H, dtype=jnp.int32)[:, None, None]
    col_ids = jnp.arange(GRID_W, dtype=jnp.int32)[None, :, None]
    row_gap = row_ids - center_rows[None, None, :]
    col_gap = col_ids - center_cols[None, None, :]
    inside = jnp.any(row_gap * row_gap + col_gap * col_gap <= (radii * radii)[None, None, :], axis=2)
    kept_cells = jax.random.randint(subkeys[3], (GRID_H, GRID_W), 0, 8) != 0
    result = jnp.logical_and(inside, kept_cells).astype(jnp.int32)
    return result.at[center_rows[0], center_cols[0]].set(1)


def draw_agent_tokens(key, part):
    subkeys = jax.random.split(key, 1)
    return jnp.clip(3.0 * jax.random.normal(subkeys[0], (AGENTS, D), jnp.float32), -18.0, 18.0).astype(jnp.bfloat16)


def shard_levels(rng, shape, cuts, low, high):
    factor_of, own = 1.0, jax.random.fold_in(rng, 6)
    for axis_at, parts in cuts:
        heights = jnp.exp(jax.random.uniform(jax.random.fold_in(own, axis_at), (parts,), jnp.float32, low / len(cuts), high / len(cuts)))
        factor_of = factor_of * jnp.repeat(heights, shape[axis_at] // parts).reshape([-1 if axis == axis_at else 1 for axis in range(len(shape))])
    return factor_of


def bell_draw(own_key, extent, scale, reach, cuts=(), held_as=jnp.bfloat16):
    values = scale * jax.random.normal(own_key, extent, jnp.float32)
    if cuts:
        values = values * shard_levels(own_key, extent, cuts, -0.22, 0.18)
    return jnp.clip(values, -reach, reach).astype(held_as)


def setup_inputs(seed: int = 0, part: int = 0) -> dict:
    keys = jax.random.split(jax.random.key(seed), 11)
    part_splits = jax.random.split(jax.random.fold_in(keys[10], part), 11)
    return {
        "patches": bell_draw(part_splits[0], (GRID_H, GRID_W, D), 1.0, 6.0, ((0, 16),)),
        "tissue": draw_tissue(jax.random.fold_in(jax.random.fold_in(keys[10], part), 71), part),
        "w_query": bell_draw(keys[2], (D, D), D ** -0.5, 0.25),
        "w_key": bell_draw(keys[3], (D, D), D ** -0.5, 0.25),
        "w_value": bell_draw(keys[4], (D, D), D ** -0.5, 0.25),
        "w_out": bell_draw(keys[5], (D, D), D ** -0.5, 0.25),
        "agent_tokens": draw_agent_tokens(jax.random.fold_in(keys[10], 71), part),
        "kernel_seven": bell_draw(keys[7], (7, 7, D), 49 ** -0.5, 0.875, (), jnp.float32),
        "kernel_five": bell_draw(keys[8], (5, 5, D), 25 ** -0.5, 1.25, (), jnp.float32),
        "kernel_three": bell_draw(keys[9], (3, 3, D), 9 ** -0.5, 2.0, (), jnp.float32),
    }


def depthwise(extended, kernel, reach_rows, band_rows, grid_width):
    padded = jnp.pad(extended.astype(jnp.float32), ((0, 0), (reach_rows, reach_rows), (0, 0)))
    span_taps = kernel.shape[0]
    total = jnp.zeros((band_rows, grid_width, kernel.shape[2]), jnp.float32)
    for row_tap in range(span_taps):
        for col_tap in range(span_taps):
            total = total + padded[row_tap:row_tap + band_rows, col_tap:col_tap + grid_width] * kernel[row_tap, col_tap]
    return total


def reference(patches, tissue, w_query, w_key, w_value, w_out, agent_tokens, kernel_seven, kernel_five, kernel_three):
    score_scale = HEAD_DIM ** -0.5
    band_tokens = ROWS_DEV * GRID_W
    flat_tokens = patches.reshape(-1, D)
    queries = jnp.dot(flat_tokens, w_query, preferred_element_type=jnp.float32).astype(jnp.bfloat16)
    keys_all = jnp.dot(flat_tokens, w_key, preferred_element_type=jnp.float32).astype(jnp.bfloat16)
    values_all = jnp.dot(flat_tokens, w_value, preferred_element_type=jnp.float32).astype(jnp.bfloat16)
    agent_heads = agent_tokens.astype(jnp.float32).reshape(AGENTS, HEADS, HEAD_DIM)
    tissue_flat = tissue.reshape(-1)
    band_ids = jnp.arange(N_COL, dtype=jnp.int32)

    def band_stats(band_index):
        start = (band_index * band_tokens).astype(jnp.int32)
        key_band = lax.dynamic_slice_in_dim(keys_all, start, band_tokens, 0).astype(jnp.float32).reshape(band_tokens, HEADS, HEAD_DIM)
        value_band = lax.dynamic_slice_in_dim(values_all, start, band_tokens, 0).astype(jnp.float32).reshape(band_tokens, HEADS, HEAD_DIM)
        valid_band = lax.dynamic_slice_in_dim(tissue_flat, start, band_tokens, 0)[None, None, :] > 0
        scores = jnp.einsum('ahd,thd->hat', agent_heads, key_band) * score_scale
        peak_band = jnp.max(jnp.where(valid_band, scores, -1e30), axis=2)
        expo = jnp.where(valid_band, jnp.exp(scores - peak_band[:, :, None]), jnp.float32(0.0))
        total_band = jnp.sum(expo, axis=2)
        weighted_band = jnp.einsum('hat,thd->had', expo.astype(jnp.bfloat16).astype(jnp.float32), value_band)
        return peak_band, total_band, weighted_band

    band_peaks, band_totals, band_weighted = lax.map(band_stats, band_ids)
    peak = jnp.max(band_peaks, axis=0)
    factor = jnp.exp(band_peaks - peak[None])
    totals = jnp.sum(band_totals * factor, axis=0)
    weighted = jnp.sum(band_weighted * factor[..., None], axis=0)
    agent_values = (weighted / totals[..., None]).astype(jnp.bfloat16)

    value_grid = values_all.reshape(GRID_H, GRID_W, D)
    value_padded = jnp.pad(value_grid, ((3, 3), (0, 0), (0, 0)))

    def band_output(band_index):
        start = (band_index * band_tokens).astype(jnp.int32)
        query_band = lax.dynamic_slice_in_dim(queries, start, band_tokens, 0).astype(jnp.float32).reshape(band_tokens, HEADS, HEAD_DIM)
        scores = jnp.einsum('thd,ahd->tha', query_band, agent_heads) * score_scale
        top_score = jnp.max(scores, axis=2, keepdims=True)
        expo = jnp.exp(scores - top_score)
        token_weights = (expo / jnp.sum(expo, axis=2, keepdims=True)).astype(jnp.bfloat16)
        attended = jnp.einsum('tha,had->thd', token_weights.astype(jnp.float32), agent_values.astype(jnp.float32)).reshape(ROWS_DEV, GRID_W, D)
        extended = lax.dynamic_slice_in_dim(value_padded, (band_index * ROWS_DEV).astype(jnp.int32), ROWS_DEV + 6, 0)
        position = depthwise(extended, kernel_seven, 3, ROWS_DEV, GRID_W)
        position = position + depthwise(extended[1:-1], kernel_five, 2, ROWS_DEV, GRID_W)
        position = position + depthwise(extended[2:-2], kernel_three, 1, ROWS_DEV, GRID_W)
        blended = (attended + position).astype(jnp.bfloat16).reshape(band_tokens, D)
        return jnp.dot(blended, w_out, preferred_element_type=jnp.float32).astype(jnp.bfloat16).reshape(ROWS_DEV, GRID_W, D)

    return lax.map(band_output, band_ids).reshape(GRID_H, GRID_W, D)
```

```python
import functools

import jax
import jax.numpy as jnp
from jax import lax
from jax.experimental import pallas as pl
from jax.experimental.pallas import tpu as pltpu
from jax.sharding import PartitionSpec as P

HEADS = 8
LANES = 128
NONE = -1e30
F32, BF16 = jnp.float32, jnp.bfloat16
NT = (((1,), (1,)), ((), ()))
VMEM = pl.BlockSpec(memory_space=pltpu.VMEM)
LIMIT = 56 * 1024 * 1024


def low_half(shape):
    return lax.broadcasted_iota(jnp.int32, shape, len(shape) - 1) < LANES // 2


def head_agents(ag_ref, head):
    start = head // 2 * LANES
    pair = ag_ref[:, start : start + LANES].astype(F32) * 0.125
    keep = low_half(pair.shape)
    keep = keep if head % 2 == 0 else jnp.logical_not(keep)
    return jnp.where(keep, pair, 0.0).astype(BF16)


def stats_kernel(x_ref, tissue_ref, wk_ref, wv_ref, ag_ref, v_ref, st_ref, k_ref):
    tokens, dim = x_ref.shape
    chunk = 256
    for c in range(0, tokens, chunk):
        x = x_ref[c : c + chunk, :]
        k_ref[c : c + chunk, :] = jnp.dot(x, wk_ref[...], preferred_element_type=F32).astype(BF16)
        v_ref[c : c + chunk, :] = jnp.dot(x, wv_ref[...], preferred_element_type=F32).astype(BF16)
    rows = tissue_ref.shape[0]
    tissue = jnp.concatenate([tissue_ref[r : r + 1, :] for r in range(rows)], axis=1) > 0
    agents = ag_ref.shape[0]
    lane = lax.broadcasted_iota(jnp.int32, (agents, LANES), 1)
    side = jnp.zeros((agents, LANES), F32)
    for pair in range(HEADS // 2):
        start = pair * LANES
        got = []
        for head in (2 * pair, 2 * pair + 1):
            s = lax.dot_general(
                head_agents(ag_ref, head), k_ref[:, start : start + LANES], NT, preferred_element_type=F32
            )
            s = jnp.where(tissue, s, NONE)
            top = jnp.max(s, axis=1, keepdims=True)
            e = jnp.exp(s - jnp.maximum(top, 0.1 * NONE))
            total = jnp.sum(e, axis=1, keepdims=True)
            got.append(
                jnp.dot(e.astype(BF16), v_ref[:, start : start + LANES], preferred_element_type=F32)
            )
            side = jnp.where(lane == head, top, side)
            side = jnp.where(lane == HEADS + head, total, side)
        st_ref[:, start : start + LANES] = jnp.where(lane < LANES // 2, got[0], got[1])
    st_ref[:, dim : dim + LANES] = side


def token_side(x_ref, wq_ref, ag_ref, tw_ref):
    tokens = x_ref.shape[0]
    chunk = 256
    for c in range(0, tokens, chunk):
        q = jnp.dot(x_ref[c : c + chunk, :], wq_ref[...], preferred_element_type=F32).astype(BF16)
        for head in range(HEADS):
            start = head // 2 * LANES
            s = lax.dot_general(
                head_agents(ag_ref, head), q[:, start : start + LANES], NT, preferred_element_type=F32
            )
            e = jnp.exp(s - jnp.max(s, axis=0, keepdims=True))
            share = 1.0 / jnp.sum(e, axis=0, keepdims=True)
            tw_ref[head, :, c : c + chunk] = (e * share).astype(BF16)


def spread_taps(k7_ref, k5_ref, k3_ref, taps_ref):
    for block in range(taps_ref.shape[0]):
        at = slice(block * LANES, block * LANES + LANES)
        for p in range(7):
            for q in range(7):
                tap = k7_ref[p, q : q + 1, at]
                if 1 <= p <= 5 and 1 <= q <= 5:
                    tap = tap + k5_ref[p - 1, q - 1 : q, at]
                if 2 <= p <= 4 and 2 <= q <= 4:
                    tap = tap + k3_ref[p - 2, q - 2 : q - 1, at]
                taps_ref[block, p * 7 + q, :, :] = jnp.broadcast_to(tap, (8, LANES))


def fill_own(v_ref, ext_ref):
    blocks, ext_rows, _, _ = ext_ref.shape
    width = v_ref.shape[1]
    for block in range(blocks):
        at = slice(block * LANES, block * LANES + LANES)
        for r in range(ext_rows):
            ext_ref[block, r, 0:8, :] = jnp.zeros((8, LANES), F32)
            ext_ref[block, r, width + 8 : width + 16, :] = jnp.zeros((8, LANES), F32)
        for r in range(ext_rows - 6):
            ext_ref[block, r + 3, 8 : width + 8, :] = v_ref[r, :, at].astype(F32)


def fill_rim(rim_ref, ext_ref, first, there):
    width = rim_ref.shape[1]
    for block in range(ext_ref.shape[0]):
        at = slice(block * LANES, block * LANES + LANES)
        for r in range(3):
            rim = rim_ref[r, :, at].astype(F32)
            ext_ref[block, first + r, 8 : width + 8, :] = jnp.where(there, rim, 0.0)


def convolve(ext_ref, taps_ref, pos_ref):
    blocks, ext_rows, _, _ = ext_ref.shape
    _, rows, width, _ = pos_ref.shape
    step = 16

    def one(i, carry):
        block = i // (width // step)
        c = pl.multiple_of(i % (width // step) * step, step)
        sums = [jnp.zeros((step, LANES), F32) for _ in range(rows)]
        for q in range(7):
            taps = [jnp.concatenate([taps_ref[block, p * 7 + q]] * (step // 8), axis=0) for p in range(7)]
            for r in range(ext_rows):
                x = ext_ref[block, r, pl.ds(c + (5 + q), step), :]
                for out in range(max(r - 6, 0), min(r + 1, rows)):
                    sums[out] = sums[out] + x * taps[r - out]
        for out in range(rows):
            pos_ref[block, out, pl.ds(c, step), :] = sums[out]
        return carry

    lax.fori_loop(0, blocks * (width // step), one, 0)


def finish(av, tw_ref, pos_ref, wo_ref, out_ref):
    av_t = av.T
    blocks, _, width, _ = pos_ref.shape
    chunk = 256
    for c in range(0, out_ref.shape[0], chunk):
        parts = []
        for head in range(HEADS):
            parts.append(
                jnp.dot(
                    av_t[head * 64 : head * 64 + 64, :],
                    tw_ref[head, :, c : c + chunk],
                    preferred_element_type=F32,
                )
            )
        attended = jnp.concatenate(parts, axis=0).T
        position = jnp.concatenate(
            [
                jnp.concatenate([pos_ref[b, r] for b in range(blocks)], axis=1)
                for r in range(c // width, (c + chunk) // width)
            ],
            axis=0,
        )
        blended = (attended + position).astype(BF16)
        out_ref[c : c + chunk, :] = jnp.dot(blended, wo_ref[...], preferred_element_type=F32).astype(BF16)


def combine(got_ref, dim):
    side = got_ref[:, :, dim : dim + LANES]
    factor = jnp.exp(side - jnp.max(side, axis=0, keepdims=True))
    shape = side.shape
    keep = low_half(shape)

    def spread(x, left):
        a = jnp.broadcast_to(x[:, :, left : left + 1], shape)
        b = jnp.broadcast_to(x[:, :, left + 1 : left + 2], shape)
        return jnp.where(keep, a, b)

    parts = []
    for pair in range(HEADS // 2):
        f = spread(factor, 2 * pair)
        total = jnp.sum(f * spread(side, HEADS + 2 * pair), axis=0)
        weighted = jnp.sum(f * got_ref[:, :, pair * LANES : pair * LANES + LANES], axis=0)
        parts.append(weighted / total)
    return jnp.concatenate(parts, axis=1).astype(BF16)


class Exchange:
    def __init__(self, n, v_ref, st_ref, av_ref, above_ref, below_ref, got_ref, sems):
        self.n, self.me = n, lax.axis_index("col")
        self.v, self.st, self.av, self.got = v_ref, st_ref, av_ref, got_ref
        s1, r1, s2, r2, s3, r3 = sems
        me = self.me
        self.to = [lax.rem(me + k, n) for k in range(1, n)]
        self.source = [lax.rem(me + n - k, n) for k in range(1, n)]
        rows = v_ref.shape[0]

        def remote(src, dst, s, r, peer):
            return pltpu.make_async_remote_copy(
                src_ref=src, dst_ref=dst, send_sem=s, recv_sem=r,
                device_id={"col": peer}, device_id_type=pl.DeviceIdType.MESH,
            )

        self.scatter = [
            remote(st_ref.at[p], got_ref.at[me], s1.at[k], r1.at[k], p) for k, p in enumerate(self.to)
        ]
        self.gather = [
            remote(av_ref.at[me], av_ref.at[me], s2.at[k], r2.at[k], p) for k, p in enumerate(self.to)
        ]
        self.down = remote(v_ref.at[pl.ds(rows - 3, 3)], above_ref, s3.at[0], r3.at[0], lax.rem(me + 1, n))
        self.up = remote(v_ref.at[pl.ds(0, 3)], below_ref, s3.at[1], r3.at[1], lax.rem(me + n - 1, n))

    def enter(self):
        barrier = pltpu.get_barrier_semaphore()
        for p in self.to:
            pl.semaphore_signal(
                barrier, inc=1, device_id={"col": p}, device_id_type=pl.DeviceIdType.MESH
            )
        pl.semaphore_wait(barrier, self.n - 1)

    def start(self):
        for copy in self.scatter:
            copy.start()

        @pl.when(self.me < self.n - 1)
        def _():
            self.down.start()

        @pl.when(self.me > 0)
        def _():
            self.up.start()

        self.got[self.me] = self.st[self.me]

    def reduce(self):
        for copy in self.scatter:
            copy.wait()
        self.av[self.me] = combine(self.got, self.v.shape[2])
        for copy in self.gather:
            copy.start()

    def rims(self):
        @pl.when(self.me < self.n - 1)
        def _():
            self.down.wait_send()
            self.up.wait_recv()

        @pl.when(self.me > 0)
        def _():
            self.down.wait_recv()
            self.up.wait_send()

    def end(self):
        for copy in self.gather:
            copy.wait()


def sem_shapes(n):
    dma = pltpu.SemaphoreType.DMA
    return [dma((n - 1,)), dma((n - 1,)), dma((n - 1,)), dma((n - 1,)), dma((2,)), dma((2,))]


def rest_kernel(
    n, x_ref, wq_ref, wo_ref, ag_ref, k7_ref, k5_ref, k3_ref, v_ref, st_ref,
    out_ref, av_ref, above_ref, below_ref, got_ref, tw_ref, taps_ref, ext_ref, pos_ref, *sems
):
    work = Exchange(n, v_ref, st_ref, av_ref, above_ref, below_ref, got_ref, sems)
    above_ref[...] = jnp.zeros(above_ref.shape, BF16)
    below_ref[...] = jnp.zeros(below_ref.shape, BF16)
    work.enter()
    work.start()
    spread_taps(k7_ref, k5_ref, k3_ref, taps_ref)
    fill_own(v_ref, ext_ref)
    token_side(x_ref, wq_ref, ag_ref, tw_ref)
    work.reduce()
    work.rims()
    fill_rim(above_ref, ext_ref, 0, True)
    fill_rim(below_ref, ext_ref, ext_ref.shape[1] - 3, True)
    convolve(ext_ref, taps_ref, pos_ref)
    work.end()
    av = jnp.concatenate([av_ref[i] for i in range(n)], axis=0)
    finish(av, tw_ref, pos_ref, wo_ref, out_ref)


def on_device(n, patches, tissue, w_query, w_key, w_value, w_out, agent_tokens, k7, k5, k3):
    rows, width, dim = patches.shape
    tokens = rows * width
    agents = agent_tokens.shape[0]
    own = agents // n
    x = patches.reshape(tokens, dim)
    values, stats = pl.pallas_call(
        stats_kernel,
        out_shape=(
            jax.ShapeDtypeStruct((tokens, dim), BF16),
            jax.ShapeDtypeStruct((agents, dim + LANES), F32),
        ),
        in_specs=[VMEM] * 5,
        out_specs=(VMEM, VMEM),
        scratch_shapes=[pltpu.VMEM((tokens, dim), BF16)],
        compiler_params=pltpu.CompilerParams(vmem_limit_bytes=LIMIT),
    )(x, tissue, w_key, w_value, agent_tokens)
    values = values.reshape(rows, width, dim)
    stats = stats.reshape(n, own, dim + LANES)
    rim = (3, width, dim)
    blocks = dim // LANES
    work = [
        pltpu.VMEM((HEADS, agents, tokens), BF16),
        pltpu.VMEM((blocks, 49, 8, LANES), F32),
        pltpu.VMEM((blocks, rows + 6, width + 16, LANES), F32),
        pltpu.VMEM((blocks, rows, width, LANES), F32),
    ]
    out = pl.pallas_call(
        functools.partial(rest_kernel, n),
        out_shape=jax.ShapeDtypeStruct((tokens, dim), BF16),
        in_specs=[VMEM] * 9,
        out_specs=VMEM,
        scratch_shapes=[
            pltpu.VMEM((n, own, dim), BF16),
            pltpu.VMEM(rim, BF16),
            pltpu.VMEM(rim, BF16),
            pltpu.VMEM((n, own, dim + LANES), F32),
        ]
        + work
        + sem_shapes(n),
        compiler_params=pltpu.CompilerParams(
            vmem_limit_bytes=LIMIT, collective_id=0, has_side_effects=True
        ),
    )(x, w_query, w_out, agent_tokens, k7, k5, k3, values, stats)
    return out.reshape(rows, width, dim)


def solution(mesh):
    rows = P(("slide", "col"), None, None)
    return jax.shard_map(
        functools.partial(on_device, mesh.shape["col"]),
        mesh=mesh,
        in_specs=(rows, P(("slide", "col"), None)) + (P(),) * 8,
        out_specs=rows,
        check_vma=False,
    )
```

```python
import functools

import jax
import jax.numpy as jnp
from jax import lax
from jax.experimental import pallas as pl
from jax.experimental.pallas import tpu as pltpu
from jax.sharding import PartitionSpec as P

HEADS = 8
LANES = 128
NONE = -1e30
F32, BF16 = jnp.float32, jnp.bfloat16
NT = (((1,), (1,)), ((), ()))
VMEM = pl.BlockSpec(memory_space=pltpu.VMEM)
LIMIT = 56 * 1024 * 1024


def low_half(shape):
    return lax.broadcasted_iota(jnp.int32, shape, len(shape) - 1) < LANES // 2


def head_agents(ag_ref, head):
    start = head // 2 * LANES
    pair = ag_ref[:, start : start + LANES].astype(F32) * 0.125
    keep = low_half(pair.shape)
    keep = keep if head % 2 == 0 else jnp.logical_not(keep)
    return jnp.where(keep, pair, 0.0).astype(BF16)


def project(x_ref, w_ref, out_ref):
    width = out_ref.shape[1]
    chunk = 256
    for c in range(0, x_ref.shape[0], chunk):
        y = jnp.dot(x_ref[c : c + chunk, :], w_ref[...], preferred_element_type=F32).astype(BF16)
        for r in range(chunk // width):
            out_ref[c // width + r, :, :] = y[r * width : (r + 1) * width, :]


def band_stats(tissue_ref, ag_ref, k_ref, v_ref, st_ref):
    rows, width, dim = v_ref.shape
    tokens = rows * width
    n, own, _ = st_ref.shape
    tissue = jnp.concatenate([tissue_ref[r : r + 1, :] for r in range(rows)], axis=1) > 0
    agents = ag_ref.shape[0]
    lane = lax.broadcasted_iota(jnp.int32, (agents, LANES), 1)
    side = jnp.zeros((agents, LANES), F32)

    def put(value, start):
        for i in range(n):
            st_ref[i, :, start : start + LANES] = value[i * own : (i + 1) * own, :]

    for pair in range(HEADS // 2):
        start = pair * LANES
        keys = k_ref[:, :, start : start + LANES].reshape(tokens, LANES)
        vals = v_ref[:, :, start : start + LANES].reshape(tokens, LANES)
        got = []
        for head in (2 * pair, 2 * pair + 1):
            s = lax.dot_general(head_agents(ag_ref, head), keys, NT, preferred_element_type=F32)
            s = jnp.where(tissue, s, NONE)
            top = jnp.max(s, axis=1, keepdims=True)
            e = jnp.exp(s - jnp.maximum(top, 0.1 * NONE))
            total = jnp.sum(e, axis=1, keepdims=True)
            got.append(jnp.dot(e.astype(BF16), vals, preferred_element_type=F32))
            side = jnp.where(lane == head, top, side)
            side = jnp.where(lane == HEADS + head, total, side)
        put(jnp.where(lane < LANES // 2, got[0], got[1]), start)
    put(side, dim)


def token_side(x_ref, wq_ref, ag_ref, tw_ref):
    tokens = x_ref.shape[0]
    chunk = 256
    for c in range(0, tokens, chunk):
        q = jnp.dot(x_ref[c : c + chunk, :], wq_ref[...], preferred_element_type=F32).astype(BF16)
        for head in range(HEADS):
            start = head // 2 * LANES
            s = lax.dot_general(
                head_agents(ag_ref, head), q[:, start : start + LANES], NT, preferred_element_type=F32
            )
            e = jnp.exp(s - jnp.max(s, axis=0, keepdims=True))
            share = 1.0 / jnp.sum(e, axis=0, keepdims=True)
            tw_ref[head, :, c : c + chunk] = (e * share).astype(BF16)


def spread_taps(k7_ref, k5_ref, k3_ref, taps_ref):
    for block in range(taps_ref.shape[0]):
        at = slice(block * LANES, block * LANES + LANES)
        for p in range(7):
            for q in range(7):
                tap = k7_ref[p, q : q + 1, at]
                if 1 <= p <= 5 and 1 <= q <= 5:
                    tap = tap + k5_ref[p - 1, q - 1 : q, at]
                if 2 <= p <= 4 and 2 <= q <= 4:
                    tap = tap + k3_ref[p - 2, q - 2 : q - 1, at]
                taps_ref[block, p * 7 + q, :, :] = jnp.broadcast_to(tap, (8, LANES))


def fill_own(v_ref, ext_ref):
    blocks, ext_rows, _, _ = ext_ref.shape
    width = v_ref.shape[1]
    for block in range(blocks):
        at = slice(block * LANES, block * LANES + LANES)
        for r in range(ext_rows):
            ext_ref[block, r, 0:8, :] = jnp.zeros((8, LANES), F32)
            ext_ref[block, r, width + 8 : width + 16, :] = jnp.zeros((8, LANES), F32)
        for r in range(ext_rows - 6):
            ext_ref[block, r + 3, 8 : width + 8, :] = v_ref[r, :, at].astype(F32)


def fill_rim(rim_ref, ext_ref, first):
    width = rim_ref.shape[1]
    for block in range(ext_ref.shape[0]):
        at = slice(block * LANES, block * LANES + LANES)
        for r in range(3):
            ext_ref[block, first + r, 8 : width + 8, :] = rim_ref[r, :, at].astype(F32)


def convolve(ext_ref, taps_ref, pos_ref, part, parts):
    blocks, ext_rows, _, _ = ext_ref.shape
    _, rows, width, _ = pos_ref.shape
    step = 16

    def one(i, carry):
        block = i // (width // step)
        c = pl.multiple_of(i % (width // step) * step, step)
        sums = [jnp.zeros((step, LANES), F32) for _ in range(rows)]
        for q in range(7):
            taps = [jnp.concatenate([taps_ref[block, p * 7 + q]] * (step // 8), axis=0) for p in range(7)]
            for r in range(ext_rows):
                x = ext_ref[block, r, pl.ds(c + (5 + q), step), :]
                for out in range(max(r - 6, 0), min(r + 1, rows)):
                    sums[out] = sums[out] + x * taps[r - out]
        for out in range(rows):
            pos_ref[block, out, pl.ds(c, step), :] = sums[out]
        return carry

    steps = blocks * (width // step)
    lax.fori_loop(part * steps // parts, (part + 1) * steps // parts, one, 0)


def blend(av, tw_ref, pos_ref, out_ref):
    av_t = av.T
    blocks, _, width, _ = pos_ref.shape
    chunk = 256
    for c in range(0, out_ref.shape[0], chunk):
        parts = []
        for head in range(HEADS):
            parts.append(
                jnp.dot(
                    av_t[head * 64 : head * 64 + 64, :],
                    tw_ref[head, :, c : c + chunk],
                    preferred_element_type=F32,
                )
            )
        attended = jnp.concatenate(parts, axis=0).T
        position = jnp.concatenate(
            [
                jnp.concatenate([pos_ref[b, r] for b in range(blocks)], axis=1)
                for r in range(c // width, (c + chunk) // width)
            ],
            axis=0,
        )
        out_ref[c : c + chunk, :] = (attended + position).astype(BF16)


def combine(got_ref, dim):
    side = got_ref[:, :, dim : dim + LANES]
    factor = jnp.exp(side - jnp.max(side, axis=0, keepdims=True))
    shape = side.shape
    keep = low_half(shape)

    def spread(x, left):
        a = jnp.broadcast_to(x[:, :, left : left + 1], shape)
        b = jnp.broadcast_to(x[:, :, left + 1 : left + 2], shape)
        return jnp.where(keep, a, b)

    parts = []
    for pair in range(HEADS // 2):
        f = spread(factor, 2 * pair)
        total = jnp.sum(f * spread(side, HEADS + 2 * pair), axis=0)
        weighted = jnp.sum(f * got_ref[:, :, pair * LANES : pair * LANES + LANES], axis=0)
        parts.append(weighted / total)
    return jnp.concatenate(parts, axis=1).astype(BF16)


class Exchange:
    def __init__(self, n, v_ref, st_ref, av_ref, above_ref, below_ref, got_ref, sems):
        self.n, self.me = n, lax.axis_index("col")
        self.v, self.st, self.av, self.got = v_ref, st_ref, av_ref, got_ref
        s1, r1, s2, r2, s3, r3 = sems
        me = self.me
        self.to = [lax.rem(me + k, n) for k in range(1, n)]
        self.source = [lax.rem(me + n - k, n) for k in range(1, n)]
        rows = v_ref.shape[0]

        def remote(src, dst, s, r, peer):
            return pltpu.make_async_remote_copy(
                src_ref=src, dst_ref=dst, send_sem=s, recv_sem=r,
                device_id={"col": peer}, device_id_type=pl.DeviceIdType.MESH,
            )

        self.scatter = [
            remote(st_ref.at[p], got_ref.at[me], s1.at[k], r1.at[k], p) for k, p in enumerate(self.to)
        ]
        self.gather = [
            remote(av_ref.at[me], av_ref.at[me], s2.at[k], r2.at[k], p) for k, p in enumerate(self.to)
        ]
        self.down = remote(v_ref.at[pl.ds(rows - 3, 3)], above_ref, s3.at[0], r3.at[0], lax.rem(me + 1, n))
        self.up = remote(v_ref.at[pl.ds(0, 3)], below_ref, s3.at[1], r3.at[1], lax.rem(me + n - 1, n))

    def greet(self):
        barrier = pltpu.get_barrier_semaphore()
        for p in self.to:
            pl.semaphore_signal(
                barrier, inc=1, device_id={"col": p}, device_id_type=pl.DeviceIdType.MESH
            )

    def met(self):
        pl.semaphore_wait(pltpu.get_barrier_semaphore(), self.n - 1)

    def send_rims(self):
        @pl.when(self.me < self.n - 1)
        def _():
            self.down.start()

        @pl.when(self.me > 0)
        def _():
            self.up.start()

    def send_stats(self):
        for copy in self.scatter:
            copy.start()
        self.got[self.me] = self.st[self.me]

    def reduce(self):
        for copy in self.scatter:
            copy.wait()
        self.av[self.me] = combine(self.got, self.v.shape[2])
        for copy in self.gather:
            copy.start()

    def rims(self):
        @pl.when(self.me < self.n - 1)
        def _():
            self.down.wait_send()
            self.up.wait_recv()

        @pl.when(self.me > 0)
        def _():
            self.down.wait_recv()
            self.up.wait_send()

    def end(self):
        for copy in self.gather:
            copy.wait()


def sem_shapes(n):
    dma = pltpu.SemaphoreType.DMA
    return [dma((n - 1,)), dma((n - 1,)), dma((n - 1,)), dma((n - 1,)), dma((2,)), dma((2,))]


def whole_kernel(
    n, x_ref, tissue_ref, wq_ref, wk_ref, wv_ref, ag_ref, k7_ref, k5_ref, k3_ref, out_ref,
    v_ref, k_ref, st_ref, av_ref, above_ref, below_ref, got_ref, tw_ref, taps_ref, ext_ref, pos_ref, *sems
):
    work = Exchange(n, v_ref, st_ref, av_ref, above_ref, below_ref, got_ref, sems)
    above_ref[...] = jnp.zeros(above_ref.shape, BF16)
    below_ref[...] = jnp.zeros(below_ref.shape, BF16)
    work.greet()
    project(x_ref, wv_ref, v_ref)
    work.met()
    work.send_rims()
    project(x_ref, wk_ref, k_ref)
    band_stats(tissue_ref, ag_ref, k_ref, v_ref, st_ref)
    work.send_stats()
    spread_taps(k7_ref, k5_ref, k3_ref, taps_ref)
    fill_own(v_ref, ext_ref)
    token_side(x_ref, wq_ref, ag_ref, tw_ref)
    work.rims()
    fill_rim(above_ref, ext_ref, 0)
    fill_rim(below_ref, ext_ref, ext_ref.shape[1] - 3)
    convolve(ext_ref, taps_ref, pos_ref, 0, 2)
    work.reduce()
    convolve(ext_ref, taps_ref, pos_ref, 1, 2)
    work.end()
    av = jnp.concatenate([av_ref[i] for i in range(n)], axis=0)
    blend(av, tw_ref, pos_ref, out_ref)


def on_device(n, patches, tissue, w_query, w_key, w_value, w_out, agent_tokens, k7, k5, k3):
    rows, width, dim = patches.shape
    tokens = rows * width
    agents = agent_tokens.shape[0]
    own = agents // n
    x = patches.reshape(tokens, dim)
    rim = (3, width, dim)
    blocks = dim // LANES
    blended = pl.pallas_call(
        functools.partial(whole_kernel, n),
        out_shape=jax.ShapeDtypeStruct((tokens, dim), BF16),
        in_specs=[VMEM] * 9,
        out_specs=VMEM,
        scratch_shapes=[
            pltpu.VMEM((rows, width, dim), BF16),
            pltpu.VMEM((rows, width, dim), BF16),
            pltpu.VMEM((n, own, dim + LANES), F32),
            pltpu.VMEM((n, own, dim), BF16),
            pltpu.VMEM(rim, BF16),
            pltpu.VMEM(rim, BF16),
            pltpu.VMEM((n, own, dim + LANES), F32),
            pltpu.VMEM((HEADS, agents, tokens), BF16),
            pltpu.VMEM((blocks, 49, 8, LANES), F32),
            pltpu.VMEM((blocks, rows + 6, width + 16, LANES), F32),
            pltpu.VMEM((blocks, rows, width, LANES), F32),
        ]
        + sem_shapes(n),
        compiler_params=pltpu.CompilerParams(
            vmem_limit_bytes=LIMIT, collective_id=0, has_side_effects=True
        ),
    )(x, tissue, w_query, w_key, w_value, agent_tokens, k7, k5, k3)
    mixed = jnp.dot(blended, w_out, preferred_element_type=F32).astype(BF16)
    return mixed.reshape(rows, width, dim)


def solution(mesh):
    rows = P(("slide", "col"), None, None)
    return jax.shard_map(
        functools.partial(on_device, mesh.shape["col"]),
        mesh=mesh,
        in_specs=(rows, P(("slide", "col"), None)) + (P(),) * 8,
        out_specs=rows,
        check_vma=False,
    )
```

```python
import functools

import jax
import jax.numpy as jnp
from jax import lax
from jax.experimental import pallas as pl
from jax.experimental.pallas import tpu as pltpu
from jax.sharding import PartitionSpec as P

HEADS = 8
LANES = 128
NONE = -1e30
F32, BF16 = jnp.float32, jnp.bfloat16
NT = (((1,), (1,)), ((), ()))
VMEM = pl.BlockSpec(memory_space=pltpu.VMEM)
LIMIT = 56 * 1024 * 1024


def low_half(shape):
    return lax.broadcasted_iota(jnp.int32, shape, len(shape) - 1) < LANES // 2


def head_agents(ag_ref, head):
    start = head // 2 * LANES
    pair = ag_ref[:, start : start + LANES].astype(F32) * 0.125
    keep = low_half(pair.shape)
    keep = keep if head % 2 == 0 else jnp.logical_not(keep)
    return jnp.where(keep, pair, 0.0).astype(BF16)


def split_agents(ag_ref, heads_ref):
    for head in range(HEADS):
        heads_ref[head, :, :] = head_agents(ag_ref, head)


def project_values(x_ref, w_ref, out_ref, ext_ref):
    rows, width, dim = out_ref.shape
    chunk = 256
    for c in range(0, x_ref.shape[0], chunk):
        y = jnp.dot(x_ref[c : c + chunk, :], w_ref[...], preferred_element_type=F32).astype(BF16)
        wide = y.astype(F32)
        for r in range(chunk // width):
            row = c // width + r
            out_ref[row, :, :] = y[r * width : (r + 1) * width, :]
            for block in range(dim // LANES):
                ext_ref[block, row + 3, 8 : width + 8, :] = wide[
                    r * width : (r + 1) * width, block * LANES : (block + 1) * LANES
                ]


def project(x_ref, w_ref, out_ref):
    width = out_ref.shape[1]
    chunk = 256
    for c in range(0, x_ref.shape[0], chunk):
        y = jnp.dot(x_ref[c : c + chunk, :], w_ref[...], preferred_element_type=F32).astype(BF16)
        for r in range(chunk // width):
            out_ref[c // width + r, :, :] = y[r * width : (r + 1) * width, :]


def band_stats(tissue_ref, heads_ref, k_ref, v_ref, st_ref):
    rows, width, dim = v_ref.shape
    tokens = rows * width
    n, own, _ = st_ref.shape
    tissue = jnp.concatenate([tissue_ref[r : r + 1, :] for r in range(rows)], axis=1) > 0
    agents = heads_ref.shape[1]
    lane = lax.broadcasted_iota(jnp.int32, (agents, LANES), 1)
    side = jnp.zeros((agents, LANES), F32)

    def put(value, start):
        for i in range(n):
            st_ref[i, :, start : start + LANES] = value[i * own : (i + 1) * own, :]

    for pair in range(HEADS // 2):
        start = pair * LANES
        keys = k_ref[:, :, start : start + LANES].reshape(tokens, LANES)
        vals = v_ref[:, :, start : start + LANES].reshape(tokens, LANES)
        got = []
        for head in (2 * pair, 2 * pair + 1):
            s = lax.dot_general(heads_ref[head], keys, NT, preferred_element_type=F32)
            s = jnp.where(tissue, s, NONE)
            top = jnp.max(s, axis=1, keepdims=True)
            e = jnp.exp(s - jnp.maximum(top, 0.1 * NONE))
            total = jnp.sum(e, axis=1, keepdims=True)
            got.append(jnp.dot(e.astype(BF16), vals, preferred_element_type=F32))
            side = jnp.where(lane == head, top, side)
            side = jnp.where(lane == HEADS + head, total, side)
        put(jnp.where(lane < LANES // 2, got[0], got[1]), start)
    put(side, dim)


def token_side(x_ref, wq_ref, heads_ref, tw_ref):
    tokens = x_ref.shape[0]
    chunk = 256
    for c in range(0, tokens, chunk):
        q = jnp.dot(x_ref[c : c + chunk, :], wq_ref[...], preferred_element_type=F32).astype(BF16)
        for head in range(HEADS):
            start = head // 2 * LANES
            s = lax.dot_general(
                heads_ref[head], q[:, start : start + LANES], NT, preferred_element_type=F32
            )
            e = jnp.exp(s - jnp.max(s, axis=0, keepdims=True))
            share = 1.0 / jnp.sum(e, axis=0, keepdims=True)
            tw_ref[head, :, c : c + chunk] = (e * share).astype(BF16)


def spread_taps(k7_ref, k5_ref, k3_ref, taps_ref):
    for block in range(taps_ref.shape[0]):
        at = slice(block * LANES, block * LANES + LANES)
        for p in range(7):
            for q in range(7):
                tap = k7_ref[p, q : q + 1, at]
                if 1 <= p <= 5 and 1 <= q <= 5:
                    tap = tap + k5_ref[p - 1, q - 1 : q, at]
                if 2 <= p <= 4 and 2 <= q <= 4:
                    tap = tap + k3_ref[p - 2, q - 2 : q - 1, at]
                taps_ref[block, p * 7 + q, :, :] = jnp.broadcast_to(tap, (8, LANES))


def fill_sides(ext_ref):
    blocks, ext_rows, padded, _ = ext_ref.shape
    for block in range(blocks):
        for r in range(ext_rows):
            ext_ref[block, r, 0:8, :] = jnp.zeros((8, LANES), F32)
            ext_ref[block, r, padded - 8 : padded, :] = jnp.zeros((8, LANES), F32)


def fill_rim(rim_ref, ext_ref, first):
    width = rim_ref.shape[1]
    for block in range(ext_ref.shape[0]):
        at = slice(block * LANES, block * LANES + LANES)
        for r in range(3):
            ext_ref[block, first + r, 8 : width + 8, :] = rim_ref[r, :, at].astype(F32)


def convolve(ext_ref, taps_ref, pos_ref, part, parts):
    blocks, ext_rows, _, _ = ext_ref.shape
    _, rows, width, _ = pos_ref.shape
    step = 8

    def one(block, carry):
        for c in range(0, width, step):
            sums = [None] * rows
            for q in range(7):
                taps = [taps_ref[block, p * 7 + q] for p in range(7)]
                for r in range(ext_rows):
                    x = ext_ref[block, r, c + 5 + q : c + 5 + q + step, :]
                    for out in range(max(r - 6, 0), min(r + 1, rows)):
                        term = x * taps[r - out]
                        sums[out] = term if sums[out] is None else sums[out] + term
            for out in range(rows):
                pos_ref[block, out, c : c + step, :] = sums[out]
        return carry

    lax.fori_loop(part * blocks // parts, (part + 1) * blocks // parts, one, 0)


def blend(av, tw_ref, pos_ref, out_ref):
    av_t = av.T
    blocks, _, width, _ = pos_ref.shape
    chunk = 256
    for c in range(0, out_ref.shape[0], chunk):
        parts = []
        for head in range(HEADS):
            parts.append(
                jnp.dot(
                    av_t[head * 64 : head * 64 + 64, :],
                    tw_ref[head, :, c : c + chunk],
                    preferred_element_type=F32,
                )
            )
        attended = jnp.concatenate(parts, axis=0).T
        position = jnp.concatenate(
            [
                jnp.concatenate([pos_ref[b, r] for b in range(blocks)], axis=1)
                for r in range(c // width, (c + chunk) // width)
            ],
            axis=0,
        )
        out_ref[c : c + chunk, :] = (attended + position).astype(BF16)


def combine(got_ref, dim):
    side = got_ref[:, :, dim : dim + LANES]
    factor = jnp.exp(side - jnp.max(side, axis=0, keepdims=True))
    shape = side.shape
    keep = low_half(shape)

    def spread(x, left):
        a = jnp.broadcast_to(x[:, :, left : left + 1], shape)
        b = jnp.broadcast_to(x[:, :, left + 1 : left + 2], shape)
        return jnp.where(keep, a, b)

    parts = []
    for pair in range(HEADS // 2):
        f = spread(factor, 2 * pair)
        total = jnp.sum(f * spread(side, HEADS + 2 * pair), axis=0)
        weighted = jnp.sum(f * got_ref[:, :, pair * LANES : pair * LANES + LANES], axis=0)
        parts.append(weighted / total)
    return jnp.concatenate(parts, axis=1).astype(BF16)


class Exchange:
    def __init__(self, n, v_ref, st_ref, av_ref, above_ref, below_ref, got_ref, sems):
        self.n, self.me = n, lax.axis_index("col")
        self.v, self.st, self.av, self.got = v_ref, st_ref, av_ref, got_ref
        s1, r1, s2, r2, s3, r3 = sems
        me = self.me
        self.to = [lax.rem(me + k, n) for k in range(1, n)]
        self.source = [lax.rem(me + n - k, n) for k in range(1, n)]
        rows = v_ref.shape[0]

        def remote(src, dst, s, r, peer):
            return pltpu.make_async_remote_copy(
                src_ref=src, dst_ref=dst, send_sem=s, recv_sem=r,
                device_id={"col": peer}, device_id_type=pl.DeviceIdType.MESH,
            )

        self.scatter = [
            remote(st_ref.at[p], got_ref.at[me], s1.at[k], r1.at[k], p) for k, p in enumerate(self.to)
        ]
        self.gather = [
            remote(av_ref.at[me], av_ref.at[me], s2.at[k], r2.at[k], p) for k, p in enumerate(self.to)
        ]
        self.down = remote(v_ref.at[pl.ds(rows - 3, 3)], above_ref, s3.at[0], r3.at[0], lax.rem(me + 1, n))
        self.up = remote(v_ref.at[pl.ds(0, 3)], below_ref, s3.at[1], r3.at[1], lax.rem(me + n - 1, n))

    def greet(self):
        barrier = pltpu.get_barrier_semaphore()
        for p in self.to:
            pl.semaphore_signal(
                barrier, inc=1, device_id={"col": p}, device_id_type=pl.DeviceIdType.MESH
            )

    def met(self):
        pl.semaphore_wait(pltpu.get_barrier_semaphore(), self.n - 1)

    def send_rims(self):
        @pl.when(self.me < self.n - 1)
        def _():
            self.down.start()

        @pl.when(self.me > 0)
        def _():
            self.up.start()

    def send_stats(self):
        for copy in self.scatter:
            copy.start()
        self.got[self.me] = self.st[self.me]

    def reduce(self):
        for copy in self.scatter:
            copy.wait()
        self.av[self.me] = combine(self.got, self.v.shape[2])
        for copy in self.gather:
            copy.start()

    def rims(self):
        @pl.when(self.me < self.n - 1)
        def _():
            self.down.wait_send()
            self.up.wait_recv()

        @pl.when(self.me > 0)
        def _():
            self.down.wait_recv()
            self.up.wait_send()

    def end(self):
        for copy in self.gather:
            copy.wait()


def sem_shapes(n):
    dma = pltpu.SemaphoreType.DMA
    return [dma((n - 1,)), dma((n - 1,)), dma((n - 1,)), dma((n - 1,)), dma((2,)), dma((2,))]


def whole_kernel(n, *refs):
    sources, out_ref = refs[:9], refs[9]
    held, load_sem = refs[10:19], refs[19]
    x_ref, tissue_ref, wq_ref, wk_ref, wv_ref, ag_ref, k7_ref, k5_ref, k3_ref = held
    (v_ref, k_ref, st_ref, av_ref, above_ref, below_ref, got_ref, tw_ref, taps_ref, ext_ref, pos_ref,
     heads_ref, *sems) = refs[20:]
    loads = [pltpu.make_async_copy(sources[i], held[i], load_sem.at[i]) for i in range(9)]
    for i in (0, 4, 3, 5, 1, 6, 7, 8, 2):
        loads[i].start()
    work = Exchange(n, v_ref, st_ref, av_ref, above_ref, below_ref, got_ref, sems)
    above_ref[...] = jnp.zeros(above_ref.shape, BF16)
    below_ref[...] = jnp.zeros(below_ref.shape, BF16)
    work.greet()
    fill_sides(ext_ref)
    loads[0].wait()
    loads[4].wait()
    project_values(x_ref, wv_ref, v_ref, ext_ref)
    loads[5].wait()
    split_agents(ag_ref, heads_ref)
    work.met()
    work.send_rims()
    loads[3].wait()
    loads[1].wait()
    project(x_ref, wk_ref, k_ref)
    band_stats(tissue_ref, heads_ref, k_ref, v_ref, st_ref)
    work.send_stats()
    for i in (6, 7, 8, 2):
        loads[i].wait()
    spread_taps(k7_ref, k5_ref, k3_ref, taps_ref)
    token_side(x_ref, wq_ref, heads_ref, tw_ref)
    work.rims()
    fill_rim(above_ref, ext_ref, 0)
    fill_rim(below_ref, ext_ref, ext_ref.shape[1] - 3)
    convolve(ext_ref, taps_ref, pos_ref, 0, 2)
    work.reduce()
    convolve(ext_ref, taps_ref, pos_ref, 1, 2)
    work.end()
    av = jnp.concatenate([av_ref[i] for i in range(n)], axis=0)
    blend(av, tw_ref, pos_ref, out_ref)


def on_device(n, patches, tissue, w_query, w_key, w_value, w_out, agent_tokens, k7, k5, k3):
    rows, width, dim = patches.shape
    tokens = rows * width
    agents = agent_tokens.shape[0]
    own = agents // n
    x = patches.reshape(tokens, dim)
    rim = (3, width, dim)
    blocks = dim // LANES
    given = (x, tissue, w_query, w_key, w_value, agent_tokens, k7, k5, k3)
    blended = pl.pallas_call(
        functools.partial(whole_kernel, n),
        out_shape=jax.ShapeDtypeStruct((tokens, dim), BF16),
        in_specs=[pl.BlockSpec(memory_space=pltpu.HBM)] * len(given),
        out_specs=VMEM,
        scratch_shapes=[pltpu.VMEM(a.shape, a.dtype) for a in given]
        + [
            pltpu.SemaphoreType.DMA((len(given),)),
            pltpu.VMEM((rows, width, dim), BF16),
            pltpu.VMEM((rows, width, dim), BF16),
            pltpu.VMEM((n, own, dim + LANES), F32),
            pltpu.VMEM((n, own, dim), BF16),
            pltpu.VMEM(rim, BF16),
            pltpu.VMEM(rim, BF16),
            pltpu.VMEM((n, own, dim + LANES), F32),
            pltpu.VMEM((HEADS, agents, tokens), BF16),
            pltpu.VMEM((blocks, 49, 8, LANES), F32),
            pltpu.VMEM((blocks, rows + 6, width + 16, LANES), F32),
            pltpu.VMEM((blocks, rows, width, LANES), F32),
            pltpu.VMEM((HEADS, agents, LANES), BF16),
        ]
        + sem_shapes(n),
        compiler_params=pltpu.CompilerParams(
            vmem_limit_bytes=LIMIT, collective_id=0, has_side_effects=True
        ),
    )(*given)
    mixed = jnp.dot(blended, w_out, preferred_element_type=F32).astype(BF16)
    return mixed.reshape(rows, width, dim)


def solution(mesh):
    rows = P(("slide", "col"), None, None)
    return jax.shard_map(
        functools.partial(on_device, mesh.shape["col"]),
        mesh=mesh,
        in_specs=(rows, P(("slide", "col"), None)) + (P(),) * 8,
        out_specs=rows,
        check_vma=False,
    )
```
